32 devices in a mesh: cell: 8 (over z, x), desc: 4 (over y, core).
Axes of the slice: x: 2, y: 2, z: 4, core: 2. Of those that a mesh axis runs over, the one named last changes fastest.
Arguments:
- cells: float32 [8192, 256], P('cell'), may hold values from -128 to 128
- descs: float32 [8192, 256], P('desc'), may hold values from -4 to 4
- g_start: float32 [8192], P('desc'), may hold values from -8 to 8
- cot_f: float32 [8192], P('cell'), may hold values from -24 to 24
- cot_g: float32 [8192], P('desc'), may hold values from -24 to 24
Outputs:
- grad_cells: float32 [8192, 256], P('cell')
- grad_descs: float32 [8192, 256], P('desc')
The draws below stay inside these ranges and needn't reach their ends.
All inputs are finite; a program needn't handle non-finite values.
Results may differ from the reference program's by a relative error of at most 0.0003.
Values sent between devices are 32-bit elements; how exact they have to be, the bound alone decides.
A program may use at most 192 MiB of HBM per device.

```python
import math
import jax
import jax.numpy as jnp
from jax import lax

W = 256
ITERS = 4
CELL_DEV = 1024
DESC_DEV = 2048
NC = 8192
ND = 8192
N_CELL = 8
N_DESC = 4


def shared_embeddings(key):
    key_x = jax.random.fold_in(key, 11)
    key_y = jax.random.fold_in(key, 12)
    key_noise = jax.random.fold_in(key, 13)
    key_strength = jax.random.fold_in(key, 14)
    total_cells = CELL_DEV * N_CELL
    total_desc = DESC_DEV * N_DESC
    col_ids = jnp.arange(total_desc)
    row_ids = jnp.arange(total_cells)
    noise = jnp.clip(jax.random.normal(key_noise, (total_desc, W), jnp.float32), -4.0, 4.0)
    paired = col_ids % 64 == 1
    yvals = jnp.clip(jax.random.normal(key_y, (total_desc, W), jnp.float32), -4.0, 4.0)
    xvals = jnp.clip(jax.random.normal(key_x, (total_cells, W), jnp.float32), -4.0, 4.0)
    xvals = xvals + 2.0
    before = jnp.roll(yvals, 1, axis=0)
    yvals = jnp.where(paired[:, None], before + 0.1 * math.sqrt(W) / 16.0 * noise, yvals)
    yvals = jnp.clip(yvals, -4.0, 4.0)
    starved = col_ids % 512 == 7
    yvals = jnp.where(starved[:, None], -4.0, yvals)
    planted = row_ids % 128 == 0
    target = row_ids // 128 * 64 % total_desc
    strength = (120.0 + 180.0 * jax.random.uniform(key_strength, (total_cells,), jnp.float32)) / (2.0 * math.sqrt(W))
    xvals = jnp.where(planted[:, None], strength[:, None] * jnp.take(yvals, target, axis=0), xvals)
    return (xvals, yvals)


def draw_cells(key, part):
    return shared_embeddings(key)[0].astype(jnp.float32)


def draw_descs(key, part):
    return shared_embeddings(key)[1].astype(jnp.float32)


def block_scale(rng, shape, split, least, largest):
    factor_of, own = 1.0, jax.random.fold_in(rng, 6)
    for dim, blocks in split:
        draws = jnp.exp(jax.random.uniform(jax.random.fold_in(own, dim), (blocks,), jnp.float32, least / len(split), largest / len(split)))
        factor_of = factor_of * jnp.repeat(draws, shape[dim] // blocks).reshape([-1 if axis == dim else 1 for axis in range(len(shape))])
    return factor_of


def bell_draw(stream_key, dims, scale, most, shards=(), dtype=jnp.bfloat16):
    entries = jax.random.normal(stream_key, dims, jnp.float32) * scale
    if len(shards) > 0:
        entries = block_scale(stream_key, dims, shards, -0.22, 0.18) * entries
    return jnp.clip(entries, min=-most, max=most).astype(dtype)


def setup_inputs(seed: int = 0) -> dict:
    splits = jax.random.split(jax.random.key(seed), 6)
    return {
        "cells": draw_cells(jax.random.fold_in(splits[5], 71), 0),
        "descs": draw_descs(jax.random.fold_in(splits[5], 71), 0),
        "g_start": bell_draw(splits[2], (ND,), 2.0, 8.0, ((0, 4),), jnp.float32),
        "cot_f": bell_draw(splits[3], (NC,), 4.0, 24.0, ((0, 8),), jnp.float32),
        "cot_g": bell_draw(splits[4], (ND,), 4.0, 24.0, ((0, 4),), jnp.float32),
    }


def reference(cells, descs, g_start, cot_f, cot_g):
    scale = 2.0 / math.sqrt(W)
    highest = lax.Precision.HIGHEST
    blocks = cells.reshape(N_CELL, CELL_DEV, W)
    cf_blocks = cot_f.reshape(N_CELL, CELL_DEV)
    total_desc = descs.shape[0]

    def logits(block):
        return lax.dot_general(block, descs, (((1,), (1,)), ((), ())), precision=highest, preferred_element_type=jnp.float32) * scale
    g_now = g_start
    f_list = []
    g_list = [g_start]
    for step in range(ITERS):

        def forward(carry, block):
            col_max, col_sum = carry
            lg = logits(block)
            zvals = lg + g_now[None, :]
            row_max = lax.optimization_barrier(jnp.max(zvals, axis=1))
            f_blk = -(row_max + jnp.log(lax.optimization_barrier(jnp.sum(jnp.exp(zvals - row_max[:, None]), axis=1))))
            wvals = lg + f_blk[:, None]
            new_max = jnp.maximum(col_max, lax.optimization_barrier(jnp.max(wvals, axis=0)))
            new_sum = col_sum * jnp.exp(col_max - new_max) + lax.optimization_barrier(jnp.sum(jnp.exp(wvals - new_max[None, :]), axis=0))
            return ((new_max, new_sum), f_blk)
        start = (jnp.full((total_desc,), -jnp.inf, jnp.float32), jnp.zeros((total_desc,), jnp.float32))
        (col_max, col_sum), f_blocks = lax.scan(forward, start, blocks)
        g_now = -(col_max + jnp.log(col_sum))
        f_list.append(f_blocks)
        g_list.append(g_now)
    gbar = cot_g
    grad_x = jnp.zeros((N_CELL, CELL_DEV, W), jnp.float32)
    grad_y = jnp.zeros((total_desc, W), jnp.float32)
    for step in reversed(range(ITERS)):
        g_here = g_list[step + 1]
        ratio = jnp.exp(g_list[step] - g_here)
        final = step == ITERS - 1
        gbar_now = gbar

        def backward(carry, item):
            gsum, gy = carry
            block, f_blk, cf_blk, gx_blk = item
            lg = logits(block)
            bplan = jnp.exp(lg + f_blk[:, None] + g_here[None, :])
            fbar = -lax.optimization_barrier(jnp.sum(bplan * gbar_now[None, :], axis=1))
            if final:
                fbar = fbar + cf_blk
            aplan = bplan * ratio[None, :]
            gsum = gsum - lax.optimization_barrier(jnp.sum(aplan * fbar[:, None], axis=0))
            lbar = -(bplan * gbar_now[None, :] + aplan * fbar[:, None])
            gx_blk = gx_blk + scale * jnp.dot(lbar, descs, precision=highest, preferred_element_type=jnp.float32)
            gy = gy + scale * lax.dot_general(lbar, block, (((0,), (0,)), ((), ())), precision=highest, preferred_element_type=jnp.float32)
            return ((gsum, gy), gx_blk)
        (gsum, grad_y), grad_x = lax.scan(backward, (jnp.zeros((total_desc,), jnp.float32), grad_y), (blocks, f_list[step], cf_blocks, grad_x))
        gbar = gsum
    return (grad_x.reshape(N_CELL * CELL_DEV, W), grad_y)
```

```python
import functools
import math

import jax
import jax.numpy as jnp
from jax import lax
from jax.experimental import pallas as pl
from jax.experimental.pallas import tpu as pltpu
from jax.sharding import PartitionSpec as P

ITERS = 4
MESH = pl.DeviceIdType.MESH
LANES = 128
F32 = jnp.float32
BF16 = jnp.bfloat16


def tree(op, parts):
    parts = list(parts)
    while len(parts) > 1:
        parts = [op(parts[i], parts[i + 1]) if i + 1 < len(parts) else parts[i] for i in range(0, len(parts), 2)]
    return parts[0]


def rotate(start, offset, count):
    return lax.rem(start + offset + count, count)


def send_all(axis, count, me, buf, send_sem, recv_sem, index):
    for off in range(1, count):
        peer = rotate(me, off, count)
        pltpu.make_async_remote_copy(
            src_ref=buf.at[index, me],
            dst_ref=buf.at[index, me],
            send_sem=send_sem.at[index, off],
            recv_sem=recv_sem.at[index, me],
            device_id={axis: peer},
            device_id_type=MESH,
        ).start()


def wait_all(axis, count, me, buf, send_sem, recv_sem, index):
    for off in range(1, count):
        source = rotate(me, -off, count)
        peer = rotate(me, off, count)
        got = pltpu.make_async_remote_copy(
            src_ref=buf.at[index, source],
            dst_ref=buf.at[index, source],
            send_sem=send_sem.at[index, off],
            recv_sem=recv_sem.at[index, source],
            device_id={axis: peer},
            device_id_type=MESH,
        )
        got.wait_recv()
        got.wait_send()


def split(value):
    high = value.astype(BF16)
    return high, (value - high.astype(F32)).astype(BF16)


def dot3(a_high, a_low, b_high, b_low):
    dot = functools.partial(jnp.dot, preferred_element_type=F32)
    return dot(a_high, b_high) + (dot(a_low, b_high) + dot(a_high, b_low))


def plan_kernel(
    n_cell, n_desc,
    cells, descs, g_first, cf, cg,
    px, py,
    logit, bplan, lbar, vcol, racc_m, racc_s, cacc_m, cacc_s, wide_a, wide_b,
    f_all, g_all, gbar, d_high, d_low, c_high, c_low,
    row_buf, col_buf, fbar_buf, gbar_buf,
    row_send, row_recv, col_send, col_recv, fb_send, fb_recv, gb_send, gb_recv,
):
    rows, width = cells.shape
    cols = descs.shape[0]
    scale = 2.0 / math.sqrt(width)
    my_cell = lax.axis_index("cell")
    my_desc = lax.axis_index("desc")
    blocks = cols // LANES
    group = 16
    unroll = 4

    barrier = pltpu.get_barrier_semaphore()
    for off in range(1, n_desc):
        pl.semaphore_signal(barrier, inc=1, device_id={"desc": rotate(my_desc, off, n_desc)}, device_id_type=MESH)
    for off in range(1, n_cell):
        pl.semaphore_signal(barrier, inc=1, device_id={"cell": rotate(my_cell, off, n_cell)}, device_id_type=MESH)

    def multiply(i, _):
        at = pl.ds(pl.multiple_of(i * 256, 256), 256)
        logit[at, :] = scale * lax.dot_general(
            cells[at, :], descs[...], (((1,), (1,)), ((), ())),
            precision=lax.Precision.HIGHEST, preferred_element_type=F32,
        )
        return 0

    lax.fori_loop(0, rows // 256, multiply, 0)
    g_all[0] = g_first[...]
    gbar[...] = cg[...]
    pl.semaphore_wait(barrier, n_desc + n_cell - 2)

    def spread_rows(vector):
        vcol[...] = jnp.broadcast_to(vector, (LANES, rows)).T

    def lane(b):
        return slice(b * LANES, (b + 1) * LANES)

    def forward(k, _):
        wide_a[...] = jnp.broadcast_to(g_all[k], (8, cols))

        def row_pass(i, _):
            for u in range(unroll):
                at = pl.ds(pl.multiple_of((i * unroll + u) * 8, 8), 8)
                parts = [logit[at, lane(b)] + wide_a[:, lane(b)] for b in range(blocks)]
                top = tree(jnp.maximum, parts)
                racc_m[at, :] = top
                racc_s[at, :] = tree(jnp.add, [jnp.exp(part - top) for part in parts])
            return 0

        lax.fori_loop(0, rows // (8 * unroll), row_pass, 0)
        tops = racc_m[...].T
        top = jnp.max(tops, axis=0, keepdims=True)
        row_buf[k, my_desc, 0:1, :] = top
        row_buf[k, my_desc, 1:2, :] = jnp.sum(racc_s[...].T * jnp.exp(tops - top), axis=0, keepdims=True)
        send_all("desc", n_desc, my_desc, row_buf, row_send, row_recv, k)
        wait_all("desc", n_desc, my_desc, row_buf, row_send, row_recv, k)
        tops = [row_buf[k, p, 0:1, :] for p in range(n_desc)]
        top = tree(jnp.maximum, tops)
        total = tree(jnp.add, [row_buf[k, p, 1:2, :] * jnp.exp(tops[p] - top) for p in range(n_desc)])
        f_now = -(top + jnp.log(total))
        f_all[k] = f_now
        spread_rows(f_now)
        cacc_m[...] = jnp.full((8, cols), -jnp.inf, F32)
        cacc_s[...] = jnp.zeros((8, cols), F32)

        def col_pass(i, _):
            base = i * (8 * group)
            for b in range(blocks):
                ats = [pl.ds(pl.multiple_of(base + 8 * u, 8), 8) for u in range(group)]
                parts = [logit[at, lane(b)] + vcol[at, :] for at in ats]
                before = cacc_m[:, lane(b)]
                top = jnp.maximum(before, tree(jnp.maximum, parts))
                cacc_m[:, lane(b)] = top
                cacc_s[:, lane(b)] = cacc_s[:, lane(b)] * jnp.exp(before - top) + tree(
                    jnp.add, [jnp.exp(part - top) for part in parts]
                )
            return 0

        lax.fori_loop(0, rows // (8 * group), col_pass, 0)
        top = jnp.max(cacc_m[...], axis=0, keepdims=True)
        col_buf[k, my_cell, 0:1, :] = top
        col_buf[k, my_cell, 1:2, :] = jnp.sum(cacc_s[...] * jnp.exp(cacc_m[...] - top), axis=0, keepdims=True)
        send_all("cell", n_cell, my_cell, col_buf, col_send, col_recv, k)
        wait_all("cell", n_cell, my_cell, col_buf, col_send, col_recv, k)
        tops = [col_buf[k, p, 0:1, :] for p in range(n_cell)]
        top = tree(jnp.maximum, tops)
        total = tree(jnp.add, [col_buf[k, p, 1:2, :] * jnp.exp(tops[p] - top) for p in range(n_cell)])
        g_all[k + 1] = -(top + jnp.log(total))
        return 0

    lax.fori_loop(0, ITERS, forward, 0)

    def backward(t, _):
        k = ITERS - 1 - t
        wide_a[...] = jnp.broadcast_to(g_all[k + 1], (8, cols))
        wide_b[...] = jnp.broadcast_to(gbar[...], (8, cols))
        spread_rows(f_all[k])

        def row_pass(i, _):
            for u in range(unroll):
                at = pl.ds(pl.multiple_of((i * unroll + u) * 8, 8), 8)
                f_here = vcol[at, :]
                terms = []
                for b in range(blocks):
                    value = jnp.exp((logit[at, lane(b)] + f_here) + wide_a[:, lane(b)])
                    bplan[at, lane(b)] = value
                    terms.append(value * wide_b[:, lane(b)])
                racc_s[at, :] = tree(jnp.add, terms)
            return 0

        lax.fori_loop(0, rows // (8 * unroll), row_pass, 0)
        fbar_buf[k, my_desc] = jnp.sum(racc_s[...].T, axis=0, keepdims=True)
        send_all("desc", n_desc, my_desc, fbar_buf, fb_send, fb_recv, k)
        wait_all("desc", n_desc, my_desc, fbar_buf, fb_send, fb_recv, k)
        fbar = -tree(jnp.add, [fbar_buf[k, p] for p in range(n_desc)])
        fbar = fbar + jnp.where(t == 0, cf[...], 0.0)
        spread_rows(fbar)
        ratio = jnp.exp(g_all[k] - g_all[k + 1])
        wide_a[...] = jnp.broadcast_to(ratio, (8, cols))
        cacc_s[...] = jnp.zeros((8, cols), F32)

        def col_pass(first):
            def body(i, _):
                base = i * (8 * group)
                for b in range(blocks):
                    terms = []
                    for u in range(group):
                        at = pl.ds(pl.multiple_of(base + 8 * u, 8), 8)
                        value = bplan[at, lane(b)]
                        term = value * vcol[at, :]
                        terms.append(term)
                        update = value * wide_b[:, lane(b)] + term * wide_a[:, lane(b)]
                        lbar[at, lane(b)] = -update if first else lbar[at, lane(b)] - update
                    cacc_s[:, lane(b)] = cacc_s[:, lane(b)] + tree(jnp.add, terms)
                return 0

            lax.fori_loop(0, rows // (8 * group), body, 0)

        @pl.when(t == 0)
        def _():
            col_pass(True)

        @pl.when(t > 0)
        def _():
            col_pass(False)

        @pl.when(t < ITERS - 1)
        def _():
            gbar_buf[k, my_cell] = jnp.sum(cacc_s[...], axis=0, keepdims=True)
            send_all("cell", n_cell, my_cell, gbar_buf, gb_send, gb_recv, k)
            wait_all("cell", n_cell, my_cell, gbar_buf, gb_send, gb_recv, k)
            total = tree(jnp.add, [gbar_buf[k, p] for p in range(n_cell)])
            gbar[...] = -(jnp.exp(g_all[k] - g_all[k + 1]) * total)

        return 0

    lax.fori_loop(0, ITERS, backward, 0)

    d_high[...], d_low[...] = split(descs[...])
    c_high[...], c_low[...] = split(cells[...].T)

    def cells_side(i, _):
        at = pl.ds(pl.multiple_of(i * 256, 256), 256)
        high, low = split(lbar[at, :])
        px[at, :] = scale * dot3(high, low, d_high[...], d_low[...])
        return 0

    lax.fori_loop(0, rows // 256, cells_side, 0)

    def descs_side(i, _):
        at = pl.ds(pl.multiple_of(i * 256, 256), 256)
        high, low = split(lbar[:, at])
        py[at, :] = (scale * dot3(c_high[...], c_low[...], high, low)).T
        return 0

    lax.fori_loop(0, cols // 256, descs_side, 0)


def run_plan(n_cell, n_desc, cells, descs, g_start, cot_f, cot_g):
    rows, width = cells.shape
    cols = descs.shape[0]
    vmem = pltpu.VMEM
    dma = pltpu.SemaphoreType.DMA
    spec = pl.BlockSpec(memory_space=pltpu.VMEM)
    return pl.pallas_call(
        functools.partial(plan_kernel, n_cell, n_desc),
        out_shape=(
            jax.ShapeDtypeStruct((rows, width), F32),
            jax.ShapeDtypeStruct((cols, width), F32),
        ),
        in_specs=[spec] * 5,
        out_specs=(spec, spec),
        scratch_shapes=[
            vmem((rows, cols), F32),
            vmem((rows, cols), F32),
            vmem((rows, cols), F32),
            vmem((rows, LANES), F32),
            vmem((rows, LANES), F32),
            vmem((rows, LANES), F32),
            vmem((8, cols), F32),
            vmem((8, cols), F32),
            vmem((8, cols), F32),
            vmem((8, cols), F32),
            vmem((ITERS, 1, rows), F32),
            vmem((ITERS + 1, 1, cols), F32),
            vmem((1, cols), F32),
            vmem((cols, width), BF16),
            vmem((cols, width), BF16),
            vmem((width, rows), BF16),
            vmem((width, rows), BF16),
            vmem((ITERS, n_desc, 2, rows), F32),
            vmem((ITERS, n_cell, 2, cols), F32),
            vmem((ITERS, n_desc, 1, rows), F32),
            vmem((ITERS, n_cell, 1, cols), F32),
            dma((ITERS, n_desc)),
            dma((ITERS, n_desc)),
            dma((ITERS, n_cell)),
            dma((ITERS, n_cell)),
            dma((ITERS, n_desc)),
            dma((ITERS, n_desc)),
            dma((ITERS, n_cell)),
            dma((ITERS, n_cell)),
        ],
        compiler_params=pltpu.CompilerParams(
            collective_id=0, has_side_effects=True, vmem_limit_bytes=60 * 1024 * 1024
        ),
        name="plan",
    )(cells, descs, g_start[None, :], cot_f[None, :], cot_g[None, :])


def solution(mesh):
    n_cell = mesh.shape["cell"]
    n_desc = mesh.shape["desc"]

    def on_device(cells, descs, g_start, cot_f, cot_g):
        part_x, part_y = run_plan(n_cell, n_desc, cells, descs, g_start, cot_f, cot_g)
        return (lax.psum(part_x, "desc"), lax.psum(part_y, "cell"))

    placed = (P("cell", None), P("desc", None), P("desc"), P("cell"), P("desc"))
    return jax.shard_map(
        on_device,
        mesh=mesh,
        in_specs=placed,
        out_specs=(P("cell", None), P("desc", None)),
        check_vma=False,
    )
```

```python
import functools
import math

import jax
import jax.numpy as jnp
from jax import lax
from jax.experimental import pallas as pl
from jax.experimental.pallas import tpu as pltpu
from jax.sharding import PartitionSpec as P

ITERS = 4
MESH = pl.DeviceIdType.MESH
LANES = 128
F32 = jnp.float32
BF16 = jnp.bfloat16


def tree(op, parts):
    parts = list(parts)
    while len(parts) > 1:
        parts = [op(parts[i], parts[i + 1]) if i + 1 < len(parts) else parts[i] for i in range(0, len(parts), 2)]
    return parts[0]


def rotate(start, offset, count):
    return lax.rem(start + offset + count, count)


def send_all(axis, count, me, buf, send_sem, recv_sem, index):
    for off in range(1, count):
        peer = rotate(me, off, count)
        pltpu.make_async_remote_copy(
            src_ref=buf.at[index, me],
            dst_ref=buf.at[index, me],
            send_sem=send_sem.at[index, off],
            recv_sem=recv_sem.at[index, me],
            device_id={axis: peer},
            device_id_type=MESH,
        ).start()


def wait_all(axis, count, me, buf, send_sem, recv_sem, index):
    for off in range(1, count):
        source = rotate(me, -off, count)
        peer = rotate(me, off, count)
        got = pltpu.make_async_remote_copy(
            src_ref=buf.at[index, source],
            dst_ref=buf.at[index, source],
            send_sem=send_sem.at[index, off],
            recv_sem=recv_sem.at[index, source],
            device_id={axis: peer},
            device_id_type=MESH,
        )
        got.wait_recv()
        got.wait_send()


def split(value):
    high = value.astype(BF16)
    return high, (value - high.astype(F32)).astype(BF16)


def dot3(a_high, a_low, b_high, b_low):
    dot = functools.partial(jnp.dot, preferred_element_type=F32)
    return dot(a_high, b_high) + (dot(a_low, b_high) + dot(a_high, b_low))


def plan_kernel(
    n_cell, n_desc,
    cells, descs, g_first, cf, cg,
    px, py,
    logit, bplan, lbar, vcol, racc_m, racc_s, cacc_m, cacc_s, wide_a, wide_b,
    f_all, g_all, gbar, d_high, d_low, c_high, c_low,
    row_buf, col_buf, fbar_buf, gbar_buf,
    row_send, row_recv, col_send, col_recv, fb_send, fb_recv, gb_send, gb_recv,
    part_x, got_x, part_y, got_y, x_send, x_recv, y_send, y_recv,
):
    rows, width = cells.shape
    cols = descs.shape[0]
    scale = 2.0 / math.sqrt(width)
    my_cell = lax.axis_index("cell")
    my_desc = lax.axis_index("desc")
    blocks = cols // LANES
    x_block = rows // n_desc
    y_block = cols // n_cell
    group = 16
    unroll = 4

    barrier = pltpu.get_barrier_semaphore()
    for off in range(1, n_desc):
        pl.semaphore_signal(barrier, inc=1, device_id={"desc": rotate(my_desc, off, n_desc)}, device_id_type=MESH)
    for off in range(1, n_cell):
        pl.semaphore_signal(barrier, inc=1, device_id={"cell": rotate(my_cell, off, n_cell)}, device_id_type=MESH)

    def multiply(i, _):
        at = pl.ds(pl.multiple_of(i * 256, 256), 256)
        logit[at, :] = scale * lax.dot_general(
            cells[at, :], descs[...], (((1,), (1,)), ((), ())),
            precision=lax.Precision.HIGHEST, preferred_element_type=F32,
        )
        return 0

    lax.fori_loop(0, rows // 256, multiply, 0)
    g_all[0] = g_first[...]
    gbar[...] = cg[...]
    pl.semaphore_wait(barrier, n_desc + n_cell - 2)

    def spread_rows(vector):
        vcol[...] = jnp.broadcast_to(vector, (LANES, rows)).T

    def lane(b):
        return slice(b * LANES, (b + 1) * LANES)

    def forward(k, _):
        wide_a[...] = jnp.broadcast_to(g_all[k], (8, cols))

        def row_pass(i, _):
            for u in range(unroll):
                at = pl.ds(pl.multiple_of((i * unroll + u) * 8, 8), 8)
                parts = [logit[at, lane(b)] + wide_a[:, lane(b)] for b in range(blocks)]
                top = tree(jnp.maximum, parts)
                racc_m[at, :] = top
                racc_s[at, :] = tree(jnp.add, [jnp.exp(part - top) for part in parts])
            return 0

        lax.fori_loop(0, rows // (8 * unroll), row_pass, 0)
        tops = racc_m[...].T
        top = jnp.max(tops, axis=0, keepdims=True)
        row_buf[k, my_desc, 0:1, :] = top
        row_buf[k, my_desc, 1:2, :] = jnp.sum(racc_s[...].T * jnp.exp(tops - top), axis=0, keepdims=True)
        send_all("desc", n_desc, my_desc, row_buf, row_send, row_recv, k)
        wait_all("desc", n_desc, my_desc, row_buf, row_send, row_recv, k)
        tops = [row_buf[k, p, 0:1, :] for p in range(n_desc)]
        top = tree(jnp.maximum, tops)
        total = tree(jnp.add, [row_buf[k, p, 1:2, :] * jnp.exp(tops[p] - top) for p in range(n_desc)])
        f_now = -(top + jnp.log(total))
        f_all[k] = f_now
        spread_rows(f_now)
        cacc_m[...] = jnp.full((8, cols), -jnp.inf, F32)
        cacc_s[...] = jnp.zeros((8, cols), F32)

        def col_pass(i, _):
            base = i * (8 * group)
            for b in range(blocks):
                ats = [pl.ds(pl.multiple_of(base + 8 * u, 8), 8) for u in range(group)]
                parts = [logit[at, lane(b)] + vcol[at, :] for at in ats]
                before = cacc_m[:, lane(b)]
                top = jnp.maximum(before, tree(jnp.maximum, parts))
                cacc_m[:, lane(b)] = top
                cacc_s[:, lane(b)] = cacc_s[:, lane(b)] * jnp.exp(before - top) + tree(
                    jnp.add, [jnp.exp(part - top) for part in parts]
                )
            return 0

        lax.fori_loop(0, rows // (8 * group), col_pass, 0)
        top = jnp.max(cacc_m[...], axis=0, keepdims=True)
        col_buf[k, my_cell, 0:1, :] = top
        col_buf[k, my_cell, 1:2, :] = jnp.sum(cacc_s[...] * jnp.exp(cacc_m[...] - top), axis=0, keepdims=True)
        send_all("cell", n_cell, my_cell, col_buf, col_send, col_recv, k)
        wait_all("cell", n_cell, my_cell, col_buf, col_send, col_recv, k)
        tops = [col_buf[k, p, 0:1, :] for p in range(n_cell)]
        top = tree(jnp.maximum, tops)
        total = tree(jnp.add, [col_buf[k, p, 1:2, :] * jnp.exp(tops[p] - top) for p in range(n_cell)])
        g_all[k + 1] = -(top + jnp.log(total))
        return 0

    lax.fori_loop(0, ITERS, forward, 0)

    def backward(t, _):
        k = ITERS - 1 - t
        wide_a[...] = jnp.broadcast_to(g_all[k + 1], (8, cols))
        wide_b[...] = jnp.broadcast_to(gbar[...], (8, cols))
        spread_rows(f_all[k])

        def row_pass(i, _):
            for u in range(unroll):
                at = pl.ds(pl.multiple_of((i * unroll + u) * 8, 8), 8)
                f_here = vcol[at, :]
                terms = []
                for b in range(blocks):
                    value = jnp.exp((logit[at, lane(b)] + f_here) + wide_a[:, lane(b)])
                    bplan[at, lane(b)] = value
                    terms.append(value * wide_b[:, lane(b)])
                racc_s[at, :] = tree(jnp.add, terms)
            return 0

        lax.fori_loop(0, rows // (8 * unroll), row_pass, 0)
        fbar_buf[k, my_desc] = jnp.sum(racc_s[...].T, axis=0, keepdims=True)
        send_all("desc", n_desc, my_desc, fbar_buf, fb_send, fb_recv, k)
        wait_all("desc", n_desc, my_desc, fbar_buf, fb_send, fb_recv, k)
        fbar = -tree(jnp.add, [fbar_buf[k, p] for p in range(n_desc)])
        fbar = fbar + jnp.where(t == 0, cf[...], 0.0)
        spread_rows(fbar)
        ratio = jnp.exp(g_all[k] - g_all[k + 1])
        wide_a[...] = jnp.broadcast_to(ratio, (8, cols))
        cacc_s[...] = jnp.zeros((8, cols), F32)

        def col_pass(first):
            def body(i, _):
                base = i * (8 * group)
                for b in range(blocks):
                    terms = []
                    for u in range(group):
                        at = pl.ds(pl.multiple_of(base + 8 * u, 8), 8)
                        value = bplan[at, lane(b)]
                        term = value * vcol[at, :]
                        terms.append(term)
                        update = value * wide_b[:, lane(b)] + term * wide_a[:, lane(b)]
                        lbar[at, lane(b)] = -update if first else lbar[at, lane(b)] - update
                    cacc_s[:, lane(b)] = cacc_s[:, lane(b)] + tree(jnp.add, terms)
                return 0

            lax.fori_loop(0, rows // (8 * group), body, 0)

        @pl.when(t == 0)
        def _():
            col_pass(True)

        @pl.when(t > 0)
        def _():
            col_pass(False)

        @pl.when(t < ITERS - 1)
        def _():
            gbar_buf[k, my_cell] = jnp.sum(cacc_s[...], axis=0, keepdims=True)
            send_all("cell", n_cell, my_cell, gbar_buf, gb_send, gb_recv, k)
            wait_all("cell", n_cell, my_cell, gbar_buf, gb_send, gb_recv, k)
            total = tree(jnp.add, [gbar_buf[k, p] for p in range(n_cell)])
            gbar[...] = -(jnp.exp(g_all[k] - g_all[k + 1]) * total)

        return 0

    lax.fori_loop(0, ITERS, backward, 0)

    d_high[...], d_low[...] = split(descs[...])
    c_high[...], c_low[...] = split(cells[...].T)

    my_rows = pl.ds(pl.multiple_of(my_desc * x_block, x_block), x_block)
    my_cols = pl.ds(pl.multiple_of(my_cell * y_block, y_block), y_block)

    def y_tile(owner):
        at = pl.ds(pl.multiple_of(owner * y_block, y_block), y_block)
        high, low = split(lbar[:, at])
        return (scale * dot3(c_high[...], c_low[...], high, low)).T

    def x_tile(owner):
        at = pl.ds(pl.multiple_of(owner * x_block, x_block), x_block)
        high, low = split(lbar[at, :])
        return scale * dot3(high, low, d_high[...], d_low[...])

    def scatter_copy(axis, part, got, send_sem, recv_sem, peer, slot, off):
        return pltpu.make_async_remote_copy(
            src_ref=part.at[peer],
            dst_ref=got.at[slot],
            send_sem=send_sem.at[0, off],
            recv_sem=recv_sem.at[0, slot],
            device_id={axis: peer},
            device_id_type=MESH,
        )

    def gather_copy(axis, out, send_sem, recv_sem, peer, slot, off, size):
        at = pl.ds(pl.multiple_of(slot * size, size), size)
        return pltpu.make_async_remote_copy(
            src_ref=out.at[at],
            dst_ref=out.at[at],
            send_sem=send_sem.at[1, off],
            recv_sem=recv_sem.at[1, slot],
            device_id={axis: peer},
            device_id_type=MESH,
        )

    def send_y(off, _):
        owner = rotate(my_cell, off, n_cell)
        part_y[owner] = y_tile(owner)
        scatter_copy("cell", part_y, got_y, y_send, y_recv, owner, my_cell, off).start()
        return 0

    def send_x(off, _):
        owner = rotate(my_desc, off, n_desc)
        part_x[owner] = x_tile(owner)
        scatter_copy("desc", part_x, got_x, x_send, x_recv, owner, my_desc, off).start()
        return 0

    lax.fori_loop(1, n_cell, send_y, 0)
    lax.fori_loop(1, n_desc, send_x, 0)
    got_y[my_cell] = y_tile(my_cell)
    got_x[my_desc] = x_tile(my_desc)

    def finish_scatter(axis, count, me, part, got, send_sem, recv_sem):
        for off in range(1, count):
            peer = rotate(me, off, count)
            scatter_copy(axis, part, got, send_sem, recv_sem, peer, rotate(me, -off, count), off).wait_recv()

    def start_gather(axis, count, me, out, send_sem, recv_sem, size):
        for off in range(1, count):
            gather_copy(axis, out, send_sem, recv_sem, rotate(me, off, count), me, off, size).start()

    finish_scatter("desc", n_desc, my_desc, part_x, got_x, x_send, x_recv)
    px[my_rows, :] = tree(jnp.add, [got_x[p] for p in range(n_desc)])
    start_gather("desc", n_desc, my_desc, px, x_send, x_recv, x_block)
    finish_scatter("cell", n_cell, my_cell, part_y, got_y, y_send, y_recv)
    py[my_cols, :] = tree(jnp.add, [got_y[p] for p in range(n_cell)])
    start_gather("cell", n_cell, my_cell, py, y_send, y_recv, y_block)
    for axis, count, me, part, got, out, send_sem, recv_sem, size in (
        ("desc", n_desc, my_desc, part_x, got_x, px, x_send, x_recv, x_block),
        ("cell", n_cell, my_cell, part_y, got_y, py, y_send, y_recv, y_block),
    ):
        for off in range(1, count):
            peer = rotate(me, off, count)
            source = rotate(me, -off, count)
            gather_copy(axis, out, send_sem, recv_sem, peer, source, off, size).wait_recv()
            scatter_copy(axis, part, got, send_sem, recv_sem, peer, source, off).wait_send()
            gather_copy(axis, out, send_sem, recv_sem, peer, me, off, size).wait_send()


def run_plan(n_cell, n_desc, cells, descs, g_start, cot_f, cot_g):
    rows, width = cells.shape
    cols = descs.shape[0]
    vmem = pltpu.VMEM
    dma = pltpu.SemaphoreType.DMA
    spec = pl.BlockSpec(memory_space=pltpu.VMEM)
    return pl.pallas_call(
        functools.partial(plan_kernel, n_cell, n_desc),
        out_shape=(
            jax.ShapeDtypeStruct((rows, width), F32),
            jax.ShapeDtypeStruct((cols, width), F32),
        ),
        in_specs=[spec] * 5,
        out_specs=(spec, spec),
        scratch_shapes=[
            vmem((rows, cols), F32),
            vmem((rows, cols), F32),
            vmem((rows, cols), F32),
            vmem((rows, LANES), F32),
            vmem((rows, LANES), F32),
            vmem((rows, LANES), F32),
            vmem((8, cols), F32),
            vmem((8, cols), F32),
            vmem((8, cols), F32),
            vmem((8, cols), F32),
            vmem((ITERS, 1, rows), F32),
            vmem((ITERS + 1, 1, cols), F32),
            vmem((1, cols), F32),
            vmem((cols, width), BF16),
            vmem((cols, width), BF16),
            vmem((width, rows), BF16),
            vmem((width, rows), BF16),
            vmem((ITERS, n_desc, 2, rows), F32),
            vmem((ITERS, n_cell, 2, cols), F32),
            vmem((ITERS, n_desc, 1, rows), F32),
            vmem((ITERS, n_cell, 1, cols), F32),
            dma((ITERS, n_desc)),
            dma((ITERS, n_desc)),
            dma((ITERS, n_cell)),
            dma((ITERS, n_cell)),
            dma((ITERS, n_desc)),
            dma((ITERS, n_desc)),
            dma((ITERS, n_cell)),
            dma((ITERS, n_cell)),
            vmem((n_desc, rows // n_desc, width), F32),
            vmem((n_desc, rows // n_desc, width), F32),
            vmem((n_cell, cols // n_cell, width), F32),
            vmem((n_cell, cols // n_cell, width), F32),
            dma((2, n_desc)),
            dma((2, n_desc)),
            dma((2, n_cell)),
            dma((2, n_cell)),
        ],
        compiler_params=pltpu.CompilerParams(
            collective_id=0, has_side_effects=True, vmem_limit_bytes=60 * 1024 * 1024
        ),
        name="plan",
    )(cells, descs, g_start[None, :], cot_f[None, :], cot_g[None, :])


def solution(mesh):
    n_cell = mesh.shape["cell"]
    n_desc = mesh.shape["desc"]

    def on_device(cells, descs, g_start, cot_f, cot_g):
        return run_plan(n_cell, n_desc, cells, descs, g_start, cot_f, cot_g)

    placed = (P("cell", None), P("desc", None), P("desc"), P("cell"), P("desc"))
    return jax.shard_map(
        on_device,
        mesh=mesh,
        in_specs=placed,
        out_specs=(P("cell", None), P("desc", None)),
        check_vma=False,
    )
```
